1024 devices in a mesh: lat: 16 (over z), wave: 64 (over x, y, core).
Axes of the slice: x: 4, y: 8, z: 16, core: 2. Of those that a mesh axis runs over, the one named last changes fastest.
Arguments:
- fourier_in: bfloat16 [64, 1280, 1280], P('wave', 'lat'), may hold values from -6 to 6
- legendre: bfloat16 [640, 1280, 1281], P('wave', 'lat'), may hold values from -0.15625 to 0.15625
- quad_weights: float32 [1280], P('lat'), may hold values from 0.3 to 3
- si_coeffs: float32 [2, 8], replicated, may hold values from 0.25 to 4
- owner_table: int32 [640], replicated, may hold values from 0 to 639, each once
Outputs:
- spectral: float32 [16, 2, 640, 1281], P('lat', None, 'wave')
- fourier_out: bfloat16 [64, 1280, 1280], P('wave', 'lat')
The draws below stay inside these ranges and needn't reach their ends.
Inputs may be any that keep to these rules, and one draw needn't show every extreme that they name: owner_table is a permutation: slot s holds zonal wavenumbers owner_table[s] and 1279 - owner_table[s], so every wavenumber is held by exactly one slot.
All inputs are finite; a program needn't handle non-finite values.
Results may differ from the reference program's by a relative error of at most 0.017.
Values may be sent and summed in bfloat16 or wider, within the bound.
No kernel may reach another device: no remote copies, remote signals or barrier semaphores. Data moves between devices by JAX's collectives and lax.ppermute only.
A program may use at most 32 MiB of HBM per device.

```python
import math
import jax
import jax.numpy as jnp
from jax import lax

TRUNC = 1279
MODES = 8
M = 1280
PAIRS = 640
NP = 1281
HEMI = 1280
CHANNELS = 16
N_LAT = 16


def levels(key, dims, shards, smallest, top_value):
    level, own = 1.0, jax.random.fold_in(key, 6)
    for dim, blocks in shards:
        draws = jnp.exp(jax.random.uniform(jax.random.fold_in(own, dim), (blocks,), jnp.float32, smallest / len(shards), top_value / len(shards)))
        level = level * jnp.repeat(draws, dims[dim] // blocks).reshape([-1 if axis == dim else 1 for axis in range(len(dims))])
    return level


def gaussian(own_key, extent, scale, bound, shards=(), held_as=jnp.bfloat16):
    entries = scale * jax.random.normal(own_key, extent, jnp.float32)
    if shards:
        entries = entries * levels(own_key, extent, shards, -0.22, 0.18)
    return jnp.clip(entries, -bound, bound).astype(held_as)


def setup_inputs(seed: int = 0) -> dict:
    key_list = jax.random.split(jax.random.key(seed), 6)
    fourier_in = gaussian(key_list[0], (4 * CHANNELS, HEMI, M), 1.0, 6.0, ((0, 64), (1, 16)))
    legendre = gaussian(key_list[1], (PAIRS, HEMI, NP), HEMI ** -0.5, 0.15625, ((0, 64), (1, 16)))
    quad_weights = jnp.clip(jnp.exp(math.log(3.0) - 2.3025851 * jax.random.uniform(key_list[2], (HEMI,), jnp.float32) ** levels(key_list[2], (HEMI,), ((0, 16),), -0.2, 0.2)), 0.3, 3.0)
    si_coeffs = jnp.clip(jnp.exp(jax.random.uniform(key_list[3], (2, MODES), jnp.float32, math.log(0.25), math.log(4.0))), 0.25, 4.0)
    owner_table = jax.random.permutation(key_list[4], PAIRS).astype(jnp.int32)
    return dict(fourier_in=fourier_in, legendre=legendre, quad_weights=quad_weights, si_coeffs=si_coeffs, owner_table=owner_table)


def slot_factors(lowest):
    column = jnp.arange(NP, dtype=jnp.int32)
    first_part = column < (M - lowest)
    degree = jnp.where(first_part, lowest + column, column - 1).astype(jnp.int32)
    wave_order = jnp.where(first_part, lowest, TRUNC - lowest).astype(jnp.int32)
    parity_sign = 1.0 - 2.0 * ((degree + wave_order) % 2).astype(jnp.float32)
    part_mask = jnp.stack([first_part, jnp.logical_not(first_part)], axis=0).astype(jnp.float32)
    hemi_sign = jnp.stack([jnp.ones_like(parity_sign), parity_sign], axis=0)
    return degree, part_mask[:, None, :] * hemi_sign[None, :, :]


def reference(fourier_in, legendre, quad_weights, si_coeffs, owner_table):
    band_loops = HEMI // N_LAT
    loop_index = jnp.arange(HEMI, dtype=jnp.int32)
    wavenumber = jnp.arange(M, dtype=jnp.int32)
    carried = wavenumber[None, :] <= 2 * loop_index[:, None] + 9
    weighted = jnp.where(carried[None, :, :], fourier_in.astype(jnp.float32) * quad_weights[None, :, None], 0.0).astype(jnp.bfloat16)
    pair_order = jnp.stack([owner_table, TRUNC - owner_table], axis=1).reshape(2 * PAIRS).astype(jnp.int32)
    ordered = jnp.take(weighted, pair_order, axis=2).reshape(2, CHANNELS, 2, HEMI, PAIRS, 2)
    ordered = jnp.moveaxis(ordered, 4, 0)

    def one_slot(items):
        columns, table, lowest = items
        degree, factors = slot_factors(lowest)
        expanded = table.astype(jnp.float32)[None, None, :, :] * factors[:, :, None, :]
        blocks = columns.astype(jnp.float32).reshape(2, CHANNELS, 2, N_LAT, band_loops, 2)
        blocked = expanded.reshape(2, 2, N_LAT, band_loops, NP)
        partial_sums = jnp.einsum("hcrbjt,thbjn->cbrn", blocks, blocked, precision=lax.Precision.HIGHEST)
        rounded = lax.optimization_barrier(partial_sums.astype(jnp.bfloat16)).astype(jnp.float32)
        raw = jnp.sum(rounded, axis=1)
        fields = raw.reshape(MODES, 2, 2, NP)
        degree_f = degree.astype(jnp.float32)
        degree_scale = (degree_f * (degree_f + 1.0) / float(TRUNC * (TRUNC + 1)))[None, None, :]
        coupling = si_coeffs[0][:, None, None]
        depth = si_coeffs[1][:, None, None]
        divergence = (fields[:, 0] + coupling * degree_scale * fields[:, 1]) / (1.0 + coupling * depth * degree_scale)
        geopotential = fields[:, 1] - depth * divergence
        by_field = jnp.stack([divergence, geopotential], axis=1)
        spectral = jnp.transpose(by_field, (0, 2, 1, 3)).reshape(2 * MODES, 2, NP)
        spectral_half = lax.optimization_barrier(by_field.astype(jnp.bfloat16)).astype(jnp.float32)
        spec_c = spectral_half.reshape(CHANNELS, 2, NP)
        synthesis = jnp.einsum("crn,thjn->hcrjt", spec_c, expanded, precision=lax.Precision.HIGHEST).astype(jnp.bfloat16)
        return spectral, synthesis

    spectral_all, synthesis_all = lax.map(one_slot, (ordered, legendre, owner_table))
    spectral = jnp.transpose(spectral_all, (1, 2, 0, 3))
    synthesis = jnp.transpose(synthesis_all, (1, 2, 3, 4, 0, 5)).reshape(4 * CHANNELS, HEMI, 2 * PAIRS)
    slot_of_pair = jnp.argsort(owner_table).astype(jnp.int32)
    lower_half = wavenumber < PAIRS
    pair_index = jnp.where(lower_half, wavenumber, TRUNC - wavenumber).astype(jnp.int32)
    column_index = (2 * jnp.take(slot_of_pair, pair_index) + jnp.where(lower_half, 0, 1)).astype(jnp.int32)
    fourier_out = jnp.take(synthesis, column_index, axis=2)
    fourier_out = jnp.where(carried[None, :, :], fourier_out, jnp.zeros_like(fourier_out))
    return spectral, fourier_out
```

```python
import jax
import jax.numpy as jnp
from jax import lax
from jax.sharding import PartitionSpec as P

TRUNC = 1279
MODES = 8
M = 1280
PAIRS = 640
NP = 1281
CHANNELS = 16
WAVE = 64
SLOTS = 10
HALF = 12


def pair_layout(lowest):
    column = jnp.arange(NP, dtype=jnp.int32)
    first_part = column[None, :] < M - lowest[:, None]
    degree = jnp.where(first_part, lowest[:, None] + column[None, :], column[None, :] - 1)
    wave_order = jnp.where(first_part, lowest[:, None], TRUNC - lowest[:, None])
    parity_sign = 1.0 - 2.0 * ((degree + wave_order) % 2).astype(jnp.float32)
    part_mask = jnp.stack([first_part, jnp.logical_not(first_part)], axis=0).astype(jnp.float32)
    hemi_sign = jnp.stack([jnp.ones_like(parity_sign), parity_sign], axis=0)
    return (degree, hemi_sign[:, None, :, :] * part_mask[None, :, :, :])


def implicit_solve(raw, coupling, depth, degree):
    degree_f = degree.astype(jnp.float32)
    scale = degree_f * (degree_f + 1.0) / float(TRUNC * (TRUNC + 1))
    divergence = (raw[0] + coupling * scale * raw[1]) / (1.0 + coupling * depth * scale)
    geopotential = raw[1] - depth * divergence
    return divergence, geopotential


def body(fourier_in, legendre, quad_weights, si_coeffs, owner_table):
    lat_index = lax.axis_index("lat")
    wave_index = lax.axis_index("wave")
    band_loops = legendre.shape[1]
    loop_index = lat_index * band_loops + jnp.arange(band_loops, dtype=jnp.int32)
    wavenumber = jnp.arange(M, dtype=jnp.int32)
    carried = wavenumber[None, :] <= 2 * loop_index[:, None] + 9
    weighted = jnp.where(
        carried, fourier_in[0].astype(jnp.float32) * quad_weights[:, None], 0.0
    ).astype(jnp.bfloat16)
    low = jnp.pad(owner_table.reshape(WAVE, SLOTS), ((0, 0), (0, HALF - SLOTS)), constant_values=-1)
    order = jnp.concatenate([low, jnp.where(low < 0, -1, TRUNC - low)], axis=1).reshape(-1)
    select = (order[:, None] == wavenumber[None, :]).astype(jnp.bfloat16)
    ordered = lax.dot_general(
        select, weighted, (((1,), (1,)), ((), ())), preferred_element_type=jnp.float32
    ).astype(jnp.bfloat16).reshape(WAVE, 2 * HALF, band_loops)
    received = lax.all_to_all(ordered, "wave", split_axis=0, concat_axis=0, tiled=True)
    received = received.reshape(2, MODES, 2, 2, 2, HALF, band_loops)[:, :, :, :, :, :SLOTS]
    lowest = lax.dynamic_slice_in_dim(owner_table, wave_index * SLOTS, SLOTS, 0)
    degree, factors = pair_layout(lowest)
    partial_sums = jnp.einsum(
        "hkfrtsj,sjn,htsn->krsfn", received, legendre, factors.astype(jnp.bfloat16),
        preferred_element_type=jnp.float32,
    ).astype(jnp.bfloat16).reshape(2 * MODES, SLOTS, 2, NP)
    bands = lax.all_to_all(partial_sums, "lat", split_axis=0, concat_axis=0, tiled=True)
    raw = jnp.sum(bands.astype(jnp.float32), axis=0)
    mode = lat_index // 2
    divergence, geopotential = implicit_solve(
        (raw[:, 0], raw[:, 1]), si_coeffs[0, mode], si_coeffs[1, mode], degree
    )
    spectral = jnp.stack([divergence, geopotential], axis=0)[None]
    half = jnp.stack([divergence, geopotential], axis=1).astype(jnp.bfloat16)[None]
    gathered = lax.all_gather(half, "lat", axis=0, tiled=True)
    fields = gathered.reshape(MODES, 2, SLOTS, 2, NP)
    signed = factors.astype(jnp.bfloat16)[:, :, None, None, None] * jnp.transpose(fields, (0, 3, 1, 2, 4))[None, None]
    synthesis = jnp.einsum(
        "htkfrsn,sjn->hkfrtsj", signed, legendre, preferred_element_type=jnp.float32
    ).astype(jnp.bfloat16)
    synthesis = jnp.pad(synthesis, ((0, 0),) * 5 + ((0, HALF - SLOTS), (0, 0)))
    synthesis = synthesis.reshape(WAVE, 2 * HALF, band_loops)
    arrived = lax.all_to_all(synthesis, "wave", split_axis=0, concat_axis=0, tiled=True)
    fourier_out = lax.dot_general(
        arrived.reshape(WAVE * 2 * HALF, band_loops), select, (((0,), (0,)), ((), ())),
        preferred_element_type=jnp.float32,
    ).astype(jnp.bfloat16)
    fourier_out = jnp.where(carried, fourier_out, jnp.zeros_like(fourier_out))[None]
    return (spectral, fourier_out)


def solution(mesh):
    in_specs = (P("wave", "lat", None), P("wave", "lat", None), P("lat"), P(), P())
    out_specs = (P("lat", None, "wave", None), P("wave", "lat", None))
    return jax.shard_map(body, mesh=mesh, in_specs=in_specs, out_specs=out_specs, check_vma=False)
```

```python
import jax
import jax.numpy as jnp
from jax import lax
from jax.sharding import PartitionSpec as P

TRUNC = 1279
MODES = 8
M = 1280
PAIRS = 640
NP = 1281
CHANNELS = 16
WAVE = 64
SLOTS = 10
HALF = 12


def pair_layout(lowest):
    column = jnp.arange(NP, dtype=jnp.int32)
    first_part = column[None, :] < M - lowest[:, None]
    degree = jnp.where(first_part, lowest[:, None] + column[None, :], column[None, :] - 1)
    wave_order = jnp.where(first_part, lowest[:, None], TRUNC - lowest[:, None])
    parity_sign = 1.0 - 2.0 * ((degree + wave_order) % 2).astype(jnp.float32)
    part_mask = jnp.stack([first_part, jnp.logical_not(first_part)], axis=0).astype(jnp.float32)
    hemi_sign = jnp.stack([jnp.ones_like(parity_sign), parity_sign], axis=0)
    return (degree, hemi_sign[:, None, :, :] * part_mask[None, :, :, :])


def implicit_solve(raw, coupling, depth, degree):
    degree_f = degree.astype(jnp.float32)
    scale = degree_f * (degree_f + 1.0) / float(TRUNC * (TRUNC + 1))
    divergence = (raw[0] + coupling * scale * raw[1]) / (1.0 + coupling * depth * scale)
    geopotential = raw[1] - depth * divergence
    return divergence, geopotential


def body(fourier_in, legendre, quad_weights, si_coeffs, owner_table):
    lat_index = lax.axis_index("lat")
    wave_index = lax.axis_index("wave")
    band_loops = legendre.shape[1]
    loop_index = lat_index * band_loops + jnp.arange(band_loops, dtype=jnp.int32)
    wavenumber = jnp.arange(M, dtype=jnp.int32)
    carried = wavenumber[None, :] <= 2 * loop_index[:, None] + 9
    weighted = jnp.where(
        carried, fourier_in[0].astype(jnp.float32) * quad_weights[:, None], 0.0
    ).astype(jnp.bfloat16)
    low = jnp.pad(owner_table.reshape(WAVE, SLOTS), ((0, 0), (0, HALF - SLOTS)), constant_values=-1)
    order = jnp.concatenate([low, jnp.where(low < 0, -1, TRUNC - low)], axis=1).reshape(-1)
    select = (order[:, None] == wavenumber[None, :]).astype(jnp.bfloat16)
    ordered = lax.dot_general(
        select, weighted, (((1,), (1,)), ((), ())), preferred_element_type=jnp.float32
    ).astype(jnp.bfloat16).reshape(WAVE, 2 * HALF, band_loops)
    received = lax.all_to_all(ordered, "wave", split_axis=0, concat_axis=0, tiled=True)
    received = received.reshape(2, MODES, 2, 2, 2, HALF, band_loops)[:, :, :, :, :, :SLOTS]
    lowest = lax.dynamic_slice_in_dim(owner_table, wave_index * SLOTS, SLOTS, 0)
    degree, factors = pair_layout(lowest)
    parity = lat_index % 2
    signs = factors.astype(jnp.bfloat16)
    away = lax.dynamic_index_in_dim(received, 1 - parity, 3, keepdims=False)
    kept = lax.dynamic_index_in_dim(received, parity, 3, keepdims=False)
    passed = jnp.einsum(
        "hkftsj,sjn,htsn->ksfn", away, legendre, signs, preferred_element_type=jnp.float32
    ).astype(jnp.bfloat16)
    n_lat = MODES * 2
    from_below = lax.ppermute(passed[: MODES // 2], "lat", [(i, (i + 1) % n_lat) for i in range(n_lat)])
    from_above = lax.ppermute(passed[MODES // 2 :], "lat", [((i + 1) % n_lat, i) for i in range(n_lat)])
    own = jnp.einsum(
        "hkftsj,sjn,htsn->ksfn", kept, legendre, signs, preferred_element_type=jnp.float32
    )
    merged = jnp.concatenate([own[: MODES // 2] + from_below.astype(jnp.float32),
                              own[MODES // 2 :] + from_above.astype(jnp.float32)], axis=0).astype(jnp.bfloat16)
    same_parity = [list(range(0, n_lat, 2)), list(range(1, n_lat, 2))]
    bands = lax.all_to_all(merged, "lat", split_axis=0, concat_axis=0, tiled=True, axis_index_groups=same_parity)
    raw = jnp.sum(bands.astype(jnp.float32), axis=0)
    mode = lat_index // 2
    divergence, geopotential = implicit_solve(
        (raw[:, 0], raw[:, 1]), si_coeffs[0, mode], si_coeffs[1, mode], degree
    )
    spectral = jnp.stack([divergence, geopotential], axis=0)[None]
    half = jnp.stack([divergence, geopotential], axis=1).astype(jnp.bfloat16)[None]
    gathered = lax.all_gather(half, "lat", axis=0, tiled=True)
    fields = gathered.reshape(MODES, 2, SLOTS, 2, NP)
    signed = factors.astype(jnp.bfloat16)[:, :, None, None, None] * jnp.transpose(fields, (0, 3, 1, 2, 4))[None, None]
    synthesis = jnp.einsum(
        "htkfrsn,sjn->hkfrtsj", signed, legendre, preferred_element_type=jnp.float32
    ).astype(jnp.bfloat16)
    synthesis = jnp.pad(synthesis, ((0, 0),) * 5 + ((0, HALF - SLOTS), (0, 0)))
    synthesis = synthesis.reshape(WAVE, 2 * HALF, band_loops)
    arrived = lax.all_to_all(synthesis, "wave", split_axis=0, concat_axis=0, tiled=True)
    fourier_out = lax.dot_general(
        arrived.reshape(WAVE * 2 * HALF, band_loops), select, (((0,), (0,)), ((), ())),
        preferred_element_type=jnp.float32,
    ).astype(jnp.bfloat16)
    fourier_out = jnp.where(carried, fourier_out, jnp.zeros_like(fourier_out))[None]
    return (spectral, fourier_out)


def solution(mesh):
    in_specs = (P("wave", "lat", None), P("wave", "lat", None), P("lat"), P(), P())
    out_specs = (P("lat", None, "wave", None), P("wave", "lat", None))
    return jax.shard_map(body, mesh=mesh, in_specs=in_specs, out_specs=out_specs, check_vma=False)
```

```python
import jax
import jax.numpy as jnp
from jax import lax
from jax.sharding import PartitionSpec as P

TRUNC = 1279
MODES = 8
M = 1280
PAIRS = 640
NP = 1281
CHANNELS = 16
WAVE = 64
SLOTS = 10


def pair_layout(lowest):
    column = jnp.arange(NP, dtype=jnp.int32)
    first_part = column[None, :] < M - lowest[:, None]
    degree = jnp.where(first_part, lowest[:, None] + column[None, :], column[None, :] - 1)
    wave_order = jnp.where(first_part, lowest[:, None], TRUNC - lowest[:, None])
    parity_sign = 1.0 - 2.0 * ((degree + wave_order) % 2).astype(jnp.float32)
    part_mask = jnp.stack([first_part, jnp.logical_not(first_part)], axis=0).astype(jnp.float32)
    hemi_sign = jnp.stack([jnp.ones_like(parity_sign), parity_sign], axis=0)
    return (degree, hemi_sign[:, None, :, :] * part_mask[None, :, :, :])


def implicit_solve(raw, coupling, depth, degree):
    degree_f = degree.astype(jnp.float32)
    scale = degree_f * (degree_f + 1.0) / float(TRUNC * (TRUNC + 1))
    divergence = (raw[0] + coupling * scale * raw[1]) / (1.0 + coupling * depth * scale)
    geopotential = raw[1] - depth * divergence
    return divergence, geopotential


def body(fourier_in, legendre, quad_weights, si_coeffs, owner_table):
    lat_index = lax.axis_index("lat")
    wave_index = lax.axis_index("wave")
    band_loops = legendre.shape[1]
    loop_index = lat_index * band_loops + jnp.arange(band_loops, dtype=jnp.int32)
    wavenumber = jnp.arange(M, dtype=jnp.int32)
    carried = wavenumber[None, :] <= 2 * loop_index[:, None] + 9
    weighted = jnp.where(
        carried, fourier_in[0].astype(jnp.float32) * quad_weights[:, None], 0.0
    ).astype(jnp.bfloat16)
    low = owner_table.reshape(WAVE, SLOTS)
    order = jnp.concatenate([low, TRUNC - low], axis=1).reshape(-1)
    select = (order[:, None] == wavenumber[None, :]).astype(jnp.bfloat16)
    ordered = lax.dot_general(
        select, weighted, (((1,), (1,)), ((), ())), preferred_element_type=jnp.float32
    ).astype(jnp.bfloat16).reshape(WAVE, SLOTS, 2, band_loops)
    received = lax.all_to_all(ordered, "wave", split_axis=0, concat_axis=0, tiled=True)
    received = received.reshape(2, MODES, 2, 2, 2, SLOTS, band_loops)
    lowest = lax.dynamic_slice_in_dim(owner_table, wave_index * SLOTS, SLOTS, 0)
    degree, factors = pair_layout(lowest)
    parity = lat_index % 2
    signs = factors.astype(jnp.bfloat16)
    away = lax.dynamic_index_in_dim(received, 1 - parity, 3, keepdims=False)
    kept = lax.dynamic_index_in_dim(received, parity, 3, keepdims=False)
    passed = jnp.einsum(
        "hkftsj,sjn,htsn->ksfn", away, legendre, signs, preferred_element_type=jnp.float32
    ).astype(jnp.bfloat16)
    n_lat = MODES * 2
    from_below = lax.ppermute(passed[: MODES // 2], "lat", [(i, (i + 1) % n_lat) for i in range(n_lat)])
    from_above = lax.ppermute(passed[MODES // 2 :], "lat", [((i + 1) % n_lat, i) for i in range(n_lat)])
    own = jnp.einsum(
        "hkftsj,sjn,htsn->ksfn", kept, legendre, signs, preferred_element_type=jnp.float32
    )
    merged = jnp.concatenate([own[: MODES // 2] + from_below.astype(jnp.float32),
                              own[MODES // 2 :] + from_above.astype(jnp.float32)], axis=0).astype(jnp.bfloat16)
    same_parity = [list(range(0, n_lat, 2)), list(range(1, n_lat, 2))]
    bands = lax.all_to_all(merged, "lat", split_axis=0, concat_axis=0, tiled=True, axis_index_groups=same_parity)
    raw = jnp.sum(bands.astype(jnp.float32), axis=0)
    mode = lat_index // 2
    divergence, geopotential = implicit_solve(
        (raw[:, 0], raw[:, 1]), si_coeffs[0, mode], si_coeffs[1, mode], degree
    )
    spectral = jnp.stack([divergence, geopotential], axis=0)[None]
    half = jnp.stack([divergence, geopotential], axis=1).astype(jnp.bfloat16)[None]
    gathered = lax.all_gather(half, "lat", axis=0, tiled=True)
    fields = gathered.reshape(MODES, 2, SLOTS, 2, NP)
    signed = factors.astype(jnp.bfloat16)[:, :, None, None, None] * jnp.transpose(fields, (0, 3, 1, 2, 4))[None, None]
    synthesis = jnp.einsum(
        "htkfrsn,sjn->hkfrtsj", signed, legendre, preferred_element_type=jnp.float32
    ).astype(jnp.bfloat16)
    synthesis = synthesis.reshape(WAVE, SLOTS, 2, band_loops)
    arrived = lax.all_to_all(synthesis, "wave", split_axis=0, concat_axis=0, tiled=True)
    fourier_out = lax.dot_general(
        arrived.reshape(M, band_loops), select, (((0,), (0,)), ((), ())),
        preferred_element_type=jnp.float32,
    ).astype(jnp.bfloat16)
    fourier_out = jnp.where(carried, fourier_out, jnp.zeros_like(fourier_out))[None]
    return (spectral, fourier_out)


def solution(mesh):
    in_specs = (P("wave", "lat", None), P("wave", "lat", None), P("lat"), P(), P())
    out_specs = (P("lat", None, "wave", None), P("wave", "lat", None))
    return jax.shard_map(body, mesh=mesh, in_specs=in_specs, out_specs=out_specs, check_vma=False)
```

```python
import jax
import jax.numpy as jnp
from jax import lax
from jax.experimental import pallas as pl
from jax.experimental.pallas import tpu as pltpu
from jax.sharding import PartitionSpec as P

TRUNC = 1279
MODES = 8
M = 1280
PAIRS = 640
NP = 1281
CHANNELS = 16
WAVE = 64
SLOTS = 10
LOOPS = 80
SPLIT = MODES // 2


def pair_layout(lowest):
    column = jnp.arange(NP, dtype=jnp.int32)
    first_part = column[None, :] < M - lowest[:, None]
    degree = jnp.where(first_part, lowest[:, None] + column[None, :], column[None, :] - 1)
    wave_order = jnp.where(first_part, lowest[:, None], TRUNC - lowest[:, None])
    parity_sign = 1.0 - 2.0 * ((degree + wave_order) % 2).astype(jnp.float32)
    part_mask = jnp.stack([first_part, jnp.logical_not(first_part)], axis=0).astype(jnp.float32)
    hemi_sign = jnp.stack([jnp.ones_like(parity_sign), parity_sign], axis=0)
    return (degree, hemi_sign[:, None, :, :] * part_mask[None, :, :, :])


def implicit_solve(raw, coupling, depth, degree):
    degree_f = degree.astype(jnp.float32)
    scale = degree_f * (degree_f + 1.0) / float(TRUNC * (TRUNC + 1))
    divergence = (raw[0] + coupling * scale * raw[1]) / (1.0 + coupling * depth * scale)
    geopotential = raw[1] - depth * divergence
    return divergence, geopotential


def row_orders(owner_ref):
    row = lax.broadcasted_iota(jnp.int32, (M, 1), 0)
    upper = row % 2 == 1
    slot = row // 2
    lane = lax.broadcasted_iota(jnp.int32, (M, 128), 1)
    owner = owner_ref[...].astype(jnp.float32)
    found = jnp.zeros((M, 128), jnp.float32)
    for chunk in range(PAIRS // 128):
        found = jnp.where(lane + 128 * chunk == slot, owner[chunk : chunk + 1], found)
    low = jnp.sum(found, axis=1, keepdims=True)
    return jnp.where(upper, float(TRUNC) - low, low).astype(jnp.int32)

def one_hot(order):
    lane = lax.broadcasted_iota(jnp.int32, (M, M), 1)
    return jnp.where(lane == order, 1.0, 0.0).astype(jnp.bfloat16)

def gather_kernel(lat_ref, fourier_ref, quad_ref, owner_ref, out_ref):
    order = row_orders(owner_ref)
    moved = lax.dot_general(one_hot(order), fourier_ref[...], (((1,), (1,)), ((), ())), preferred_element_type=jnp.float32)
    loop = lat_ref[0] * LOOPS + lax.broadcasted_iota(jnp.int32, (M, LOOPS), 1)
    out_ref[...] = jnp.where(order <= 2 * loop + 9, moved * quad_ref[...], 0.0).astype(jnp.bfloat16)

def gather_rows(lat, fourier, quad, owner):
    vm = pl.BlockSpec(memory_space=pltpu.VMEM)
    return pl.pallas_call(
        gather_kernel,
        out_shape=jax.ShapeDtypeStruct((M, LOOPS), jnp.bfloat16),
        in_specs=[pl.BlockSpec(memory_space=pltpu.SMEM), vm, vm, vm],
        out_specs=vm,
        name="gather_rows",
    )(lat, fourier, quad, owner)


def body(fourier_in, legendre, quad_weights, si_coeffs, owner_table):
    lat_index = lax.axis_index("lat")
    wave_index = lax.axis_index("wave")
    band_loops = legendre.shape[1]
    loop_index = lat_index * band_loops + jnp.arange(band_loops, dtype=jnp.int32)
    wavenumber = jnp.arange(M, dtype=jnp.int32)
    carried = wavenumber[None, :] <= 2 * loop_index[:, None] + 9
    ordered = gather_rows(
        lat_index[None].astype(jnp.int32), fourier_in[0], quad_weights[None], owner_table.reshape(PAIRS // 128, 128)
    ).reshape(WAVE, SLOTS, 2, band_loops)
    received = lax.all_to_all(ordered, "wave", split_axis=0, concat_axis=0, tiled=True)
    received = received.reshape(2, MODES, 2, 2, SLOTS, 2, band_loops)
    lowest = lax.dynamic_slice_in_dim(owner_table, wave_index * SLOTS, SLOTS, 0)
    degree, factors = pair_layout(lowest)
    parity = lat_index % 2
    signs = factors.astype(jnp.bfloat16)
    away = lax.dynamic_index_in_dim(received, 1 - parity, 3, keepdims=False)
    kept = lax.dynamic_index_in_dim(received, parity, 3, keepdims=False)
    passed = jnp.einsum(
        "hkfstj,sjn,htsn->ksfn", away, legendre, signs, preferred_element_type=jnp.float32
    ).astype(jnp.bfloat16)
    n_lat = MODES * 2
    from_below = lax.ppermute(passed[:SPLIT], "lat", [(i, (i + 1) % n_lat) for i in range(n_lat)])
    from_above = lax.ppermute(passed[SPLIT:], "lat", [((i + 1) % n_lat, i) for i in range(n_lat)])
    own = jnp.einsum(
        "hkfstj,sjn,htsn->ksfn", kept, legendre, signs, preferred_element_type=jnp.float32
    )
    merged = jnp.concatenate([own[:SPLIT] + from_below.astype(jnp.float32),
                              own[SPLIT:] + from_above.astype(jnp.float32)], axis=0).astype(jnp.bfloat16)
    same_parity = [list(range(0, n_lat, 2)), list(range(1, n_lat, 2))]
    bands = lax.all_to_all(merged, "lat", split_axis=0, concat_axis=0, tiled=True, axis_index_groups=same_parity)
    raw = jnp.sum(bands.astype(jnp.float32), axis=0)
    mode = lat_index // 2
    divergence, geopotential = implicit_solve(
        (raw[:, 0], raw[:, 1]), si_coeffs[0, mode], si_coeffs[1, mode], degree
    )
    spectral = jnp.stack([divergence, geopotential], axis=0)[None]
    half = jnp.stack([divergence, geopotential], axis=1).astype(jnp.bfloat16)[None]
    gathered = lax.all_gather(half, "lat", axis=0, tiled=True)
    fields = gathered.reshape(MODES, 2, SLOTS, 2, NP)
    signed = factors.astype(jnp.bfloat16)[:, :, None, None, None] * jnp.transpose(fields, (0, 3, 1, 2, 4))[None, None]
    synthesis = jnp.einsum(
        "htkfrsn,sjn->hkfrstj", signed, legendre, preferred_element_type=jnp.float32
    ).astype(jnp.bfloat16)
    synthesis = synthesis.reshape(WAVE, SLOTS, 2, band_loops)
    arrived = lax.all_to_all(synthesis, "wave", split_axis=0, concat_axis=0, tiled=True)
    order = jnp.stack([owner_table, TRUNC - owner_table], axis=1).reshape(-1)
    select = (order[:, None] == wavenumber[None, :]).astype(jnp.bfloat16)
    fourier_out = lax.dot_general(
        arrived.reshape(M, band_loops), select, (((0,), (0,)), ((), ())),
        preferred_element_type=jnp.float32,
    ).astype(jnp.bfloat16)
    fourier_out = jnp.where(carried, fourier_out, jnp.zeros_like(fourier_out))[None]
    return (spectral, fourier_out)


def solution(mesh):
    in_specs = (P("wave", "lat", None), P("wave", "lat", None), P("lat"), P(), P())
    out_specs = (P("lat", None, "wave", None), P("wave", "lat", None))
    return jax.shard_map(body, mesh=mesh, in_specs=in_specs, out_specs=out_specs, check_vma=False)
```

```python
import jax
import jax.numpy as jnp
from jax import lax
from jax.experimental import pallas as pl
from jax.experimental.pallas import tpu as pltpu
from jax.sharding import PartitionSpec as P

TRUNC = 1279
MODES = 8
M = 1280
PAIRS = 640
NP = 1281
CHANNELS = 16
WAVE = 64
SLOTS = 10
LOOPS = 80
SPLIT = MODES // 2


def pair_layout(lowest):
    column = jnp.arange(NP, dtype=jnp.int32)
    first_part = column[None, :] < M - lowest[:, None]
    degree = jnp.where(first_part, lowest[:, None] + column[None, :], column[None, :] - 1)
    wave_order = jnp.where(first_part, lowest[:, None], TRUNC - lowest[:, None])
    parity_sign = 1.0 - 2.0 * ((degree + wave_order) % 2).astype(jnp.float32)
    part_mask = jnp.stack([first_part, jnp.logical_not(first_part)], axis=0).astype(jnp.float32)
    hemi_sign = jnp.stack([jnp.ones_like(parity_sign), parity_sign], axis=0)
    return (degree, hemi_sign[:, None, :, :] * part_mask[None, :, :, :])


def implicit_solve(raw, coupling, depth, degree):
    degree_f = degree.astype(jnp.float32)
    scale = degree_f * (degree_f + 1.0) / float(TRUNC * (TRUNC + 1))
    divergence = (raw[0] + coupling * scale * raw[1]) / (1.0 + coupling * depth * scale)
    geopotential = raw[1] - depth * divergence
    return divergence, geopotential


def row_orders(owner_ref):
    row = lax.broadcasted_iota(jnp.int32, (M, 1), 0)
    upper = row % 2 == 1
    slot = row // 2
    lane = lax.broadcasted_iota(jnp.int32, (M, 128), 1)
    owner = owner_ref[...].astype(jnp.float32)
    found = jnp.zeros((M, 128), jnp.float32)
    for chunk in range(PAIRS // 128):
        found = jnp.where(lane + 128 * chunk == slot, owner[chunk : chunk + 1], found)
    low = jnp.sum(found, axis=1, keepdims=True)
    return jnp.where(upper, float(TRUNC) - low, low).astype(jnp.int32)

def one_hot(order):
    lane = lax.broadcasted_iota(jnp.int32, (M, M), 1)
    return jnp.where(lane == order, 1.0, 0.0).astype(jnp.bfloat16)

def gather_kernel(lat_ref, fourier_ref, quad_ref, owner_ref, out_ref):
    order = row_orders(owner_ref)
    moved = lax.dot_general(one_hot(order), fourier_ref[...], (((1,), (1,)), ((), ())), preferred_element_type=jnp.float32)
    loop = lat_ref[0] * LOOPS + lax.broadcasted_iota(jnp.int32, (M, LOOPS), 1)
    out_ref[...] = jnp.where(order <= 2 * loop + 9, moved * quad_ref[...], 0.0).astype(jnp.bfloat16)

def gather_rows(lat, fourier, quad, owner):
    vm = pl.BlockSpec(memory_space=pltpu.VMEM)
    return pl.pallas_call(
        gather_kernel,
        out_shape=jax.ShapeDtypeStruct((M, LOOPS), jnp.bfloat16),
        in_specs=[pl.BlockSpec(memory_space=pltpu.SMEM), vm, vm, vm],
        out_specs=vm,
        name="gather_rows",
    )(lat, fourier, quad, owner)


def body(fourier_in, legendre, quad_weights, si_coeffs, owner_table):
    lat_index = lax.axis_index("lat")
    wave_index = lax.axis_index("wave")
    band_loops = legendre.shape[1]
    loop_index = lat_index * band_loops + jnp.arange(band_loops, dtype=jnp.int32)
    wavenumber = jnp.arange(M, dtype=jnp.int32)
    carried = wavenumber[None, :] <= 2 * loop_index[:, None] + 9
    ordered = gather_rows(
        lat_index[None].astype(jnp.int32), fourier_in[0], quad_weights[None], owner_table.reshape(PAIRS // 128, 128)
    ).reshape(WAVE, SLOTS, 2, band_loops)
    received = lax.all_to_all(ordered, "wave", split_axis=0, concat_axis=0, tiled=True)
    received = received.reshape(2, MODES, 2, 2, SLOTS, 2, band_loops)
    lowest = lax.dynamic_slice_in_dim(owner_table, wave_index * SLOTS, SLOTS, 0)
    degree, factors = pair_layout(lowest)
    parity = lat_index % 2
    signs = factors.astype(jnp.bfloat16)
    away = lax.dynamic_index_in_dim(received, 1 - parity, 3, keepdims=False)
    kept = lax.dynamic_index_in_dim(received, parity, 3, keepdims=False)
    passed = jnp.einsum(
        "hkfstj,sjn,htsn->ksfn", away, legendre, signs, preferred_element_type=jnp.float32
    ).astype(jnp.bfloat16)
    n_lat = MODES * 2
    from_below = lax.ppermute(passed[:SPLIT], "lat", [(i, (i + 1) % n_lat) for i in range(n_lat)])
    from_above = lax.ppermute(passed[SPLIT:], "lat", [((i + 1) % n_lat, i) for i in range(n_lat)])
    own = jnp.einsum(
        "hkfstj,sjn,htsn->ksfn", kept, legendre, signs, preferred_element_type=jnp.float32
    )
    incoming = jnp.concatenate([from_below, from_above], axis=0).astype(jnp.float32)
    merged = (own + incoming).astype(jnp.bfloat16)
    same_parity = [list(range(0, n_lat, 2)), list(range(1, n_lat, 2))]
    bands = lax.all_to_all(merged, "lat", split_axis=0, concat_axis=0, tiled=True, axis_index_groups=same_parity)
    raw = jnp.sum(bands.astype(jnp.float32), axis=0)
    mode = lat_index // 2
    divergence, geopotential = implicit_solve(
        (raw[:, 0], raw[:, 1]), si_coeffs[0, mode], si_coeffs[1, mode], degree
    )
    spectral = jnp.stack([divergence, geopotential], axis=0)[None]
    both = implicit_solve(
        (raw[:, :1], raw[:, 1:]), si_coeffs[0, mode], si_coeffs[1, mode], degree[:, None]
    )
    field = jnp.arange(2, dtype=jnp.int32)[None, :, None]
    half = jnp.where(field == 0, both[0], both[1]).astype(jnp.bfloat16)[None]
    gathered = lax.all_gather(half, "lat", axis=0, tiled=True)
    fields = gathered.reshape(MODES, 2, SLOTS, 2, NP)
    signed = factors.astype(jnp.bfloat16)[:, :, None, None, None] * jnp.transpose(fields, (0, 3, 1, 2, 4))[None, None]
    synthesis = jnp.einsum(
        "htkfrsn,sjn->hkfrstj", signed, legendre, preferred_element_type=jnp.float32
    ).astype(jnp.bfloat16)
    synthesis = synthesis.reshape(WAVE, SLOTS, 2, band_loops)
    arrived = lax.all_to_all(synthesis, "wave", split_axis=0, concat_axis=0, tiled=True)
    order = jnp.stack([owner_table, TRUNC - owner_table], axis=1).reshape(-1)
    select = (order[:, None] == wavenumber[None, :]).astype(jnp.bfloat16)
    fourier_out = lax.dot_general(
        arrived.reshape(M, band_loops), select, (((0,), (0,)), ((), ())),
        preferred_element_type=jnp.float32,
    ).astype(jnp.bfloat16)
    fourier_out = jnp.where(carried, fourier_out, jnp.zeros_like(fourier_out))[None]
    return (spectral, fourier_out)


def solution(mesh):
    in_specs = (P("wave", "lat", None), P("wave", "lat", None), P("lat"), P(), P())
    out_specs = (P("lat", None, "wave", None), P("wave", "lat", None))
    return jax.shard_map(body, mesh=mesh, in_specs=in_specs, out_specs=out_specs, check_vma=False)
```

```python
import jax
import jax.numpy as jnp
from jax import lax
from jax.experimental import pallas as pl
from jax.experimental.pallas import tpu as pltpu
from jax.sharding import PartitionSpec as P

TRUNC = 1279
MODES = 8
M = 1280
PAIRS = 640
NP = 1281
CHANNELS = 16
WAVE = 64
SLOTS = 10
LOOPS = 80
SPLIT = MODES // 2


def pair_layout(lowest):
    column = jnp.arange(NP, dtype=jnp.int32)
    first_part = column[None, :] < M - lowest[:, None]
    degree = jnp.where(first_part, lowest[:, None] + column[None, :], column[None, :] - 1)
    wave_order = jnp.where(first_part, lowest[:, None], TRUNC - lowest[:, None])
    parity_sign = 1.0 - 2.0 * ((degree + wave_order) % 2).astype(jnp.float32)
    part_mask = jnp.stack([first_part, jnp.logical_not(first_part)], axis=0).astype(jnp.float32)
    hemi_sign = jnp.stack([jnp.ones_like(parity_sign), parity_sign], axis=0)
    return (degree, hemi_sign[:, None, :, :] * part_mask[None, :, :, :])


def implicit_solve(raw, coupling, depth, degree):
    degree_f = degree.astype(jnp.float32)
    scale = degree_f * (degree_f + 1.0) / float(TRUNC * (TRUNC + 1))
    divergence = (raw[0] + coupling * scale * raw[1]) / (1.0 + coupling * depth * scale)
    geopotential = raw[1] - depth * divergence
    return divergence, geopotential


def row_orders(owner_ref):
    row = lax.broadcasted_iota(jnp.int32, (M, 1), 0)
    upper = row % 2 == 1
    slot = row // 2
    lane = lax.broadcasted_iota(jnp.int32, (M, 128), 1)
    owner = owner_ref[...].astype(jnp.float32)
    found = jnp.zeros((M, 128), jnp.float32)
    for chunk in range(PAIRS // 128):
        found = jnp.where(lane + 128 * chunk == slot, owner[chunk : chunk + 1], found)
    low = jnp.sum(found, axis=1, keepdims=True)
    return jnp.where(upper, float(TRUNC) - low, low).astype(jnp.int32)

def one_hot(order):
    lane = lax.broadcasted_iota(jnp.int32, (M, M), 1)
    return jnp.where(lane == order, 1.0, 0.0).astype(jnp.bfloat16)

def gather_kernel(lat_ref, fourier_ref, quad_ref, owner_ref, out_ref, held_ref, arrival):
    fetch = pltpu.make_async_copy(fourier_ref, held_ref, arrival)
    fetch.start()
    order = row_orders(owner_ref)
    fetch.wait()
    moved = lax.dot_general(
        one_hot(order), held_ref[...], (((1,), (1,)), ((), ())), preferred_element_type=jnp.float32
    )
    loop = lat_ref[0] * LOOPS + lax.broadcasted_iota(jnp.int32, (M, LOOPS), 1)
    out_ref[...] = jnp.where(order <= 2 * loop + 9, moved * quad_ref[...], 0.0).astype(jnp.bfloat16)

def gather_rows(lat, fourier, quad, owner):
    vm = pl.BlockSpec(memory_space=pltpu.VMEM)
    return pl.pallas_call(
        gather_kernel,
        out_shape=jax.ShapeDtypeStruct((M, LOOPS), jnp.bfloat16),
        in_specs=[pl.BlockSpec(memory_space=pltpu.SMEM), pl.BlockSpec(memory_space=pl.ANY), vm, vm],
        out_specs=vm,
        scratch_shapes=[pltpu.VMEM((LOOPS, M), jnp.bfloat16), pltpu.SemaphoreType.DMA],
        name="gather_rows",
    )(lat, fourier, quad, owner)


def body(fourier_in, legendre, quad_weights, si_coeffs, owner_table):
    lat_index = lax.axis_index("lat")
    wave_index = lax.axis_index("wave")
    band_loops = legendre.shape[1]
    loop_index = lat_index * band_loops + jnp.arange(band_loops, dtype=jnp.int32)
    wavenumber = jnp.arange(M, dtype=jnp.int32)
    carried = wavenumber[None, :] <= 2 * loop_index[:, None] + 9
    ordered = gather_rows(
        lat_index[None].astype(jnp.int32), fourier_in[0], quad_weights[None], owner_table.reshape(PAIRS // 128, 128)
    ).reshape(WAVE, SLOTS, 2, band_loops)
    received = lax.all_to_all(ordered, "wave", split_axis=0, concat_axis=0, tiled=True)
    received = received.reshape(2, MODES, 2, 2, SLOTS, 2, band_loops)
    lowest = lax.dynamic_slice_in_dim(owner_table, wave_index * SLOTS, SLOTS, 0)
    degree, factors = pair_layout(lowest)
    parity = lat_index % 2
    signs = factors.astype(jnp.bfloat16)
    away = lax.dynamic_index_in_dim(received, 1 - parity, 3, keepdims=False)
    kept = lax.dynamic_index_in_dim(received, parity, 3, keepdims=False)
    passed = jnp.einsum(
        "hkfstj,sjn,htsn->ksfn", away, legendre, signs, preferred_element_type=jnp.float32
    ).astype(jnp.bfloat16)
    n_lat = MODES * 2
    from_below = lax.ppermute(passed[:SPLIT], "lat", [(i, (i + 1) % n_lat) for i in range(n_lat)])
    from_above = lax.ppermute(passed[SPLIT:], "lat", [((i + 1) % n_lat, i) for i in range(n_lat)])
    own = jnp.einsum(
        "hkfstj,sjn,htsn->ksfn", kept, legendre, signs, preferred_element_type=jnp.float32
    )
    incoming = jnp.concatenate([from_below, from_above], axis=0).astype(jnp.float32)
    merged = (own + incoming).astype(jnp.bfloat16)
    same_parity = [list(range(0, n_lat, 2)), list(range(1, n_lat, 2))]
    bands = lax.all_to_all(merged, "lat", split_axis=0, concat_axis=0, tiled=True, axis_index_groups=same_parity)
    raw = jnp.sum(bands.astype(jnp.float32), axis=0)
    mode = lat_index // 2
    divergence, geopotential = implicit_solve(
        (raw[:, 0], raw[:, 1]), si_coeffs[0, mode], si_coeffs[1, mode], degree
    )
    spectral = jnp.stack([divergence, geopotential], axis=0)[None]
    both = implicit_solve(
        (raw[:, :1], raw[:, 1:]), si_coeffs[0, mode], si_coeffs[1, mode], degree[:, None]
    )
    field = jnp.arange(2, dtype=jnp.int32)[None, :, None]
    half = jnp.where(field == 0, both[0], both[1]).astype(jnp.bfloat16)[None]
    gathered = lax.all_gather(half, "lat", axis=0, tiled=True)
    fields = gathered.reshape(MODES, 2, SLOTS, 2, NP)
    signed = factors.astype(jnp.bfloat16)[:, :, None, None, None] * jnp.transpose(fields, (0, 3, 1, 2, 4))[None, None]
    synthesis = jnp.einsum(
        "htkfrsn,sjn->hkfrstj", signed, legendre, preferred_element_type=jnp.float32
    ).astype(jnp.bfloat16)
    synthesis = synthesis.reshape(WAVE, SLOTS, 2, band_loops)
    arrived = lax.all_to_all(synthesis, "wave", split_axis=0, concat_axis=0, tiled=True)
    order = jnp.stack([owner_table, TRUNC - owner_table], axis=1).reshape(-1)
    select = (order[:, None] == wavenumber[None, :]).astype(jnp.bfloat16)
    fourier_out = lax.dot_general(
        arrived.reshape(M, band_loops), select, (((0,), (0,)), ((), ())),
        preferred_element_type=jnp.float32,
    ).astype(jnp.bfloat16)
    fourier_out = jnp.where(carried, fourier_out, jnp.zeros_like(fourier_out))[None]
    return (spectral, fourier_out)


def solution(mesh):
    in_specs = (P("wave", "lat", None), P("wave", "lat", None), P("lat"), P(), P())
    out_specs = (P("lat", None, "wave", None), P("wave", "lat", None))
    return jax.shard_map(body, mesh=mesh, in_specs=in_specs, out_specs=out_specs, check_vma=False)
```
